512 devices in a mesh: dp: 2 (over core), ctx: 32 (over z, x), tp: 8 (over y).
Axes of the slice: x: 4, y: 8, z: 8, core: 2. Of those that a mesh axis runs over, the one named last changes fastest.
Arguments:
- queries: bfloat16 [8192, 16384], P(('dp', 'ctx'), 'tp'), may hold values from -6 to 6
- keys: bfloat16 [8192, 1024], P(('dp', 'ctx'), 'tp'), may hold values from -6 to 6
- values: bfloat16 [8192, 1024], P(('dp', 'ctx'), 'tp'), may hold values from -6 to 6
- output_gradient: bfloat16 [8192, 16384], P(('dp', 'ctx'), 'tp'), may hold values from -6 to 6
- doc_lens: int32 [32], replicated, may hold values from 1 to 640, 8192 in all
Outputs:
- attended: bfloat16 [8192, 16384], P(('dp', 'ctx'), 'tp')
- query_grad: bfloat16 [8192, 16384], P(('dp', 'ctx'), 'tp')
- key_gradient_rows: bfloat16 [8192, 1024], P(('dp', 'ctx'), 'tp')
- value_gradient_rows: bfloat16 [8192, 1024], P(('dp', 'ctx'), 'tp')
The draws below stay inside these ranges and needn't reach their ends.
Inputs may be any that keep to these rules, and one draw needn't show every extreme that they name: `doc_lens`: 32 lengths summing to 8192; the longest is exactly 640.
All inputs are finite; a program needn't handle non-finite values.
Results may differ from the reference program's by a relative error of at most 0.028.
Values may be sent and summed in bfloat16 or wider, within the bound.
No kernel may reach another device: no remote copies, remote signals or barrier semaphores. Data moves between devices by JAX's collectives and lax.ppermute only.
A program may use at most 64 MiB of HBM per device.

```python
import math
import jax
import jax.numpy as jnp
import numpy as np
from jax import lax

HEAD_SIZE = 128
QUERY_HEADS = 128
KEY_VALUE_HEADS = 8
BLOCK_TOKENS = 128
PACKED_TOKENS = 8192
LONGEST_DOC = 640
NDOCS = 32


def draw_queries(key, part):
    final_result = jnp.clip(jax.random.normal(jax.random.fold_in(key, 13), (PACKED_TOKENS, QUERY_HEADS, HEAD_SIZE), jnp.float32), -6.0, 6.0)
    return final_result.reshape(PACKED_TOKENS, QUERY_HEADS * HEAD_SIZE).astype(jnp.bfloat16)


def draw_keys(key, part):
    final_result = jnp.clip(jax.random.normal(jax.random.fold_in(key, 23), (PACKED_TOKENS, KEY_VALUE_HEADS, HEAD_SIZE), jnp.float32), -6.0, 6.0)
    return final_result.reshape(PACKED_TOKENS, KEY_VALUE_HEADS * HEAD_SIZE).astype(jnp.bfloat16)


def level_of(key, shape, shards, low, top_value):
    gain = 1.0
    for axis_at, parts in shards:
        draws = jax.random.uniform(jax.random.fold_in(jax.random.fold_in(key, 6), axis_at), (parts,), jnp.float32, low / len(shards), top_value / len(shards))
        gain = gain * jnp.repeat(jnp.exp(draws), shape[axis_at] // parts).reshape((-1,) + (1,) * (len(shape) - 1 - axis_at))
    return gain


def split_up(count, total, limit, skew):
    weights = [(1 << 20) // math.isqrt(grade ** skew) + 1 for grade in range(2, count + 1)]
    rest, holding = total - limit - (count - 1), [1] * (count - 1)
    while rest > 0:
        candidates = [i for i in range(count - 1) if holding[i] < limit]
        mass, remaining = sum([weights[i] for i in candidates]), rest
        for i in candidates:
            extra = min(limit - holding[i], max(1, remaining * weights[i] // mass), rest)
            holding[i] = holding[i] + extra
            rest = rest - extra
    return np.array([limit] + holding)


def uneven(rng, amount, total, limit, slope):
    if amount == 2:
        one = jax.random.randint(rng, (), max(1, total - limit), min(limit, total - 1) + 1)
        return jnp.stack([one, total - one])
    tallies = jnp.asarray(split_up(amount, total, limit, slope), jnp.int32)
    couples = (amount - 1) // 2
    donor, sink = tallies[1:1 + 2 * couples:2], tallies[2:2 + 2 * couples:2]
    margin = jnp.minimum(donor - 1, limit - sink)
    passed = jax.random.randint(jax.random.fold_in(rng, 1), (couples,), 0, 1 << 20) % (margin + 1)
    tallies = tallies.at[1:1 + 2 * couples:2].set(donor - passed).at[2:2 + 2 * couples:2].set(sink + passed)
    return tallies[jax.random.permutation(jax.random.fold_in(rng, 2), amount)]


def scatter_about(own_key, shape, scale, limit, shards=(), kind=jnp.bfloat16):
    entries = jax.random.normal(own_key, shape, jnp.float32) * scale
    if len(shards) > 0:
        entries = level_of(own_key, shape, shards, -0.22, 0.18) * entries
    return jnp.clip(entries, min=-limit, max=limit).astype(kind)


def setup_inputs(seed: int = 0) -> dict:
    arg_keys = jax.random.split(jax.random.key(seed), 6)
    return {
        "queries": draw_queries(jax.random.fold_in(arg_keys[5], 71), 0),
        "keys": draw_keys(jax.random.fold_in(arg_keys[5], 71), 0),
        "values": scatter_about(arg_keys[2], (PACKED_TOKENS, KEY_VALUE_HEADS * HEAD_SIZE), 1.0, 6.0, ((0, 64), (1, 8))),
        "output_gradient": scatter_about(arg_keys[3], (PACKED_TOKENS, QUERY_HEADS * HEAD_SIZE), 1.0, 6.0, ((0, 64), (1, 8))),
        "doc_lens": uneven(arg_keys[4], NDOCS, PACKED_TOKENS, LONGEST_DOC, 2).astype(jnp.int32),
    }


NEG = -1e30


def rounded_f32(x):
    return lax.optimization_barrier(x.astype(jnp.bfloat16)).astype(jnp.float32)


def reference(queries, keys, values, output_gradient, doc_lens):
    query_group = QUERY_HEADS // KEY_VALUE_HEADS
    scale = HEAD_SIZE ** -0.5
    ends = jnp.cumsum(doc_lens)
    positions = jnp.arange(PACKED_TOKENS, dtype=jnp.int32)
    documents = jnp.sum((positions[:, None] >= ends[None, :]).astype(jnp.int32), axis=1)
    span_rows = LONGEST_DOC + BLOCK_TOKENS
    padded_keys = jnp.concatenate([jnp.zeros((LONGEST_DOC, KEY_VALUE_HEADS * HEAD_SIZE), jnp.bfloat16), keys], 0)
    padded_values = jnp.concatenate([jnp.zeros((LONGEST_DOC, KEY_VALUE_HEADS * HEAD_SIZE), jnp.bfloat16), values], 0)
    doc_pad = jnp.concatenate([jnp.full((LONGEST_DOC,), -1, jnp.int32), documents], 0)

    def one_block(carry, block):
        key_gradients, value_gradients = carry
        start_offset = (block * BLOCK_TOKENS).astype(jnp.int32)
        query_block_rows = lax.dynamic_slice_in_dim(queries, start_offset, BLOCK_TOKENS, 0).astype(jnp.float32).reshape(BLOCK_TOKENS, KEY_VALUE_HEADS, query_group, HEAD_SIZE)
        gradient_block_rows = lax.dynamic_slice_in_dim(output_gradient, start_offset, BLOCK_TOKENS, 0).astype(jnp.float32).reshape(BLOCK_TOKENS, KEY_VALUE_HEADS, query_group, HEAD_SIZE)
        key_span_rows = lax.dynamic_slice_in_dim(padded_keys, start_offset, span_rows, 0).astype(jnp.float32).reshape(span_rows, KEY_VALUE_HEADS, HEAD_SIZE)
        value_span_rows = lax.dynamic_slice_in_dim(padded_values, start_offset, span_rows, 0).astype(jnp.float32).reshape(span_rows, KEY_VALUE_HEADS, HEAD_SIZE)
        query_doc = lax.dynamic_slice_in_dim(documents, start_offset, BLOCK_TOKENS, 0)
        key_doc = lax.dynamic_slice_in_dim(doc_pad, start_offset, span_rows, 0)
        query_pos = start_offset + jnp.arange(BLOCK_TOKENS, dtype=jnp.int32)
        key_pos = start_offset - LONGEST_DOC + jnp.arange(span_rows, dtype=jnp.int32)
        allowed = (query_doc[:, None] == key_doc[None, :]) & (key_pos[None, :] <= query_pos[:, None])
        scores = jnp.einsum("qhgd,khd->hgqk", query_block_rows, key_span_rows) * scale
        masked = jnp.where(allowed, scores, NEG)
        peak = jnp.max(masked, axis=-1)
        total = jnp.sum(jnp.where(allowed, jnp.exp(masked - peak[..., None]), 0.0), axis=-1)
        log_total = peak + jnp.log(total)
        probs = jnp.where(allowed, jnp.exp(masked - log_total[..., None]), 0.0)
        weights = rounded_f32(probs)
        attended_blk = jnp.einsum("hgqk,khd->qhgd", weights, value_span_rows).astype(jnp.bfloat16)
        delta = jnp.einsum("qhgd,qhgd->hgq", gradient_block_rows, attended_blk.astype(jnp.float32))
        spread = jnp.einsum("qhgd,khd->hgqk", gradient_block_rows, value_span_rows)
        score_grad = rounded_f32(probs * (spread - delta[..., None]) * scale)
        query_blk_grad = jnp.einsum("hgqk,khd->qhgd", score_grad, key_span_rows).astype(jnp.bfloat16)
        key_part = jnp.einsum("hgqk,qhgd->khd", score_grad, query_block_rows)
        value_part = jnp.einsum("hgqk,qhgd->khd", weights, gradient_block_rows)
        key_gradients = lax.dynamic_update_slice_in_dim(key_gradients, lax.dynamic_slice_in_dim(key_gradients, start_offset, span_rows, 0) + key_part, start_offset, 0)
        value_gradients = lax.dynamic_update_slice_in_dim(value_gradients, lax.dynamic_slice_in_dim(value_gradients, start_offset, span_rows, 0) + value_part, start_offset, 0)
        return (key_gradients, value_gradients), (attended_blk.reshape(BLOCK_TOKENS, QUERY_HEADS * HEAD_SIZE), query_blk_grad.reshape(BLOCK_TOKENS, QUERY_HEADS * HEAD_SIZE))

    zero_filled = jnp.zeros((LONGEST_DOC + PACKED_TOKENS, KEY_VALUE_HEADS, HEAD_SIZE), jnp.float32)
    blocks = jnp.arange(PACKED_TOKENS // BLOCK_TOKENS, dtype=jnp.int32)
    (key_gradients, value_gradients), (attended, query_grad) = lax.scan(one_block, (zero_filled, zero_filled), blocks)
    attended = attended.reshape(PACKED_TOKENS, QUERY_HEADS * HEAD_SIZE)
    query_grad = query_grad.reshape(PACKED_TOKENS, QUERY_HEADS * HEAD_SIZE)
    key_gradient_rows = key_gradients[LONGEST_DOC:].reshape(PACKED_TOKENS, KEY_VALUE_HEADS * HEAD_SIZE).astype(jnp.bfloat16)
    value_gradient_rows = value_gradients[LONGEST_DOC:].reshape(PACKED_TOKENS, KEY_VALUE_HEADS * HEAD_SIZE).astype(jnp.bfloat16)
    return (attended, query_grad, key_gradient_rows, value_gradient_rows)
```

```python
import jax
import jax.numpy as jnp
from jax import lax
from jax.experimental import pallas as pl
from jax.experimental.pallas import tpu as pltpu
from jax.sharding import PartitionSpec as P

HEAD = 128
TILE = 128
REACH = 5
SPAN = (REACH + 1) * TILE
SEQ_AXES = ("dp", "ctx")
SCALE = HEAD ** (-0.5)
LOG2E = 1.4426950408889634
NEG = -1e30

NT = (((1,), (1,)), ((), ()))
NN = (((1,), (0,)), ((), ()))


def dot(a, b, dims):
    return lax.dot_general(a, b, dims, preferred_element_type=jnp.float32)


def shifted(block, distance):
    devices = range(lax.axis_size(SEQ_AXES))
    route = [(i - distance, i) for i in devices if i - distance in devices]
    return lax.ppermute(block, SEQ_AXES, route)


def mask_bias(lens_ref, base, bias_ref):
    q_pos = base + REACH * TILE + lax.broadcasted_iota(jnp.int32, (8, TILE), 1)
    doc_start = jnp.zeros((8, TILE), jnp.int32)
    end = jnp.int32(0)
    for i in range(lens_ref.shape[0]):
        end = end + lens_ref[i]
        doc_start = jnp.where(q_pos >= end, jnp.maximum(doc_start, end), doc_start)
    q_pos, doc_start = q_pos[:1], doc_start[:1]
    for t in range(REACH + 1):
        k_pos = base + t * TILE + lax.broadcasted_iota(jnp.int32, (TILE, TILE), 0)
        seen = (k_pos >= doc_start) & (k_pos <= q_pos)
        bias_ref[pl.ds(t * TILE, TILE), :] = jnp.where(seen, 0.0, NEG)


def kernel(
    lens_ref, index_ref, q_ref, do_ref, far_ref, mid_ref, near_ref,
    o_ref, dq_ref, grads_ref,
    bias_ref, k_ref, v_ref, kt_ref, vt_ref, dk_ref, dv_ref,
):
    base = (index_ref[0] - REACH) * TILE
    mask_bias(lens_ref, base, bias_ref)
    for t, ref in enumerate((far_ref, mid_ref, near_ref)):
        rows = pl.ds(t * 2 * TILE, 2 * TILE)
        k = ref[:, :HEAD]
        v = ref[:, HEAD:]
        k_ref[rows, :] = k
        v_ref[rows, :] = v
        kt_ref[:, rows] = k.T
        vt_ref[:, rows] = v.T
    dk_ref[...] = jnp.zeros_like(dk_ref)
    dv_ref[...] = jnp.zeros_like(dv_ref)

    def pair(step, carry):
        at = pl.multiple_of(step * 2 * HEAD, 2 * HEAD)
        first, second = pl.ds(at, HEAD), pl.ds(pl.multiple_of(at + HEAD, HEAD), HEAD)
        q = jnp.concatenate([q_ref[:, first], q_ref[:, second]], 0)
        do = jnp.concatenate([do_ref[:, first], do_ref[:, second]], 0)
        bias = bias_ref[...]
        s = dot(k_ref[...], q, NT) * (SCALE * LOG2E) + jnp.concatenate([bias, bias], 1)
        m = jnp.max(s, axis=0, keepdims=True)
        p = jnp.exp2(s - m)
        p = p * (1.0 / jnp.sum(p, axis=0, keepdims=True))
        w = p.astype(jnp.bfloat16)
        dp = dot(v_ref[...], do, NT)
        delta = jnp.sum(p * dp, axis=0, keepdims=True)
        ds = (p * (dp - delta)).astype(jnp.bfloat16)
        dv_ref[...] += dot(w, do, NN)
        dk_ref[...] += dot(ds, q, NN)
        o = dot(vt_ref[...], w, NN).astype(jnp.bfloat16)
        dq = (dot(kt_ref[...], ds, NN) * SCALE).astype(jnp.bfloat16)
        o_ref[:, first] = o[:, :TILE].T
        o_ref[:, second] = o[:, TILE:].T
        dq_ref[:, first] = dq[:, :TILE].T
        dq_ref[:, second] = dq[:, TILE:].T
        return carry

    lax.fori_loop(0, q_ref.shape[1] // (2 * HEAD), pair, 0)
    grads_ref[:, :HEAD] = (dk_ref[...] * SCALE).astype(jnp.bfloat16)
    grads_ref[:, HEAD:] = dv_ref[...].astype(jnp.bfloat16)


def attention(lens, index, q, do, far, mid, near):
    vmem = pl.BlockSpec(memory_space=pltpu.VMEM)
    smem = pl.BlockSpec(memory_space=pltpu.SMEM)
    return pl.pallas_call(
        kernel,
        out_shape=(
            jax.ShapeDtypeStruct(q.shape, jnp.bfloat16),
            jax.ShapeDtypeStruct(q.shape, jnp.bfloat16),
            jax.ShapeDtypeStruct((SPAN, 2 * HEAD), jnp.bfloat16),
        ),
        in_specs=[smem, smem] + [vmem] * 5,
        out_specs=(vmem,) * 3,
        scratch_shapes=[
            pltpu.VMEM((SPAN, TILE), jnp.float32),
            pltpu.VMEM((SPAN, HEAD), jnp.bfloat16),
            pltpu.VMEM((SPAN, HEAD), jnp.bfloat16),
            pltpu.VMEM((HEAD, SPAN), jnp.bfloat16),
            pltpu.VMEM((HEAD, SPAN), jnp.bfloat16),
            pltpu.VMEM((SPAN, HEAD), jnp.float32),
            pltpu.VMEM((SPAN, HEAD), jnp.float32),
        ],
        compiler_params=pltpu.CompilerParams(vmem_limit_bytes=32 << 20),
        cost_estimate=pl.CostEstimate(
            flops=12 * SPAN * HEAD * q.shape[0] * (q.shape[1] // HEAD),
            transcendentals=SPAN * q.shape[0] * (q.shape[1] // HEAD),
            bytes_accessed=4 * q.size * 2 + 4 * SPAN * 2 * HEAD,
        ),
    )(lens, index, q, do, far, mid, near)


def per_device(queries, keys, values, output_gradient, doc_lens):
    index = lax.axis_index(SEQ_AXES).astype(jnp.int32)
    own = jnp.concatenate([keys, values], 1)
    before = shifted(own, 1)
    near = jnp.concatenate([before, own], 0)
    far = shifted(near, 4)
    mid = shifted(near, 2)
    attended, query_grad, grads = attention(
        doc_lens, index.reshape(1), queries, output_gradient, far, mid, near
    )
    from_far = shifted(grads[: 2 * TILE], -4).astype(jnp.float32)
    from_mid = shifted(grads[2 * TILE : 4 * TILE], -2).astype(jnp.float32)
    summed = from_far + from_mid + grads[4 * TILE :].astype(jnp.float32)
    back = shifted(summed[:TILE].astype(jnp.bfloat16), -1).astype(jnp.float32)
    total = (summed[TILE:] + back).astype(jnp.bfloat16)
    return attended, query_grad, total[:, :HEAD], total[:, HEAD:]


def solution(mesh):
    rows = P(SEQ_AXES, "tp")
    return jax.shard_map(
        per_device,
        mesh=mesh,
        in_specs=(rows, rows, rows, rows, P()),
        out_specs=(rows, rows, rows, rows),
        check_vma=False,
    )
```

```python
import functools

import jax
import jax.numpy as jnp
from jax import lax
from jax.experimental import pallas as pl
from jax.experimental.pallas import tpu as pltpu
from jax.sharding import PartitionSpec as P

HEAD = 128
TILE = 128
REACH = 5
SPAN = (REACH + 1) * TILE
CHUNK = 2 * TILE
SEQ_AXES = ("dp", "ctx")
SCALE = HEAD ** (-0.5)
LOG2E = 1.4426950408889634
NEG = -1e30
STEP = 2 * TILE

NT = (((1,), (1,)), ((), ()))
NN = (((1,), (0,)), ((), ()))
BF16 = jnp.bfloat16
F32 = jnp.float32


def dot(a, b, dims):
    return lax.dot_general(a, b, dims, preferred_element_type=F32)


def shifted(block, distance):
    devices = range(lax.axis_size(SEQ_AXES))
    route = [(i - distance, i) for i in devices if i - distance in devices]
    return lax.ppermute(block, SEQ_AXES, route)


def twice(x):
    return jnp.concatenate([x, x], 1)


def stack_kernel(
    lens_ref, index_ref, q_ref, do_ref, qs_ref, dos_ref, bias_ref, sems
):
    copies = []
    for h in range(q_ref.shape[1] // HEAD):
        part = pl.ds(h * HEAD, HEAD)
        for x, (src, dst) in enumerate(((q_ref, qs_ref), (do_ref, dos_ref))):
            copies.append(
                pltpu.make_async_copy(src.at[:, part], dst.at[part, :], sems.at[x, h])
            )
            copies[-1].start()
    base = (index_ref[0] - REACH) * TILE
    q_pos = base + REACH * TILE + lax.broadcasted_iota(jnp.int32, (8, TILE), 1)
    doc_start = jnp.zeros((8, TILE), jnp.int32)
    end = jnp.int32(0)
    for i in range(lens_ref.shape[0]):
        end = end + lens_ref[i]
        doc_start = jnp.where(q_pos >= end, jnp.maximum(doc_start, end), doc_start)
    q_pos, doc_start = q_pos[:1], doc_start[:1]
    for t in range(REACH + 1):
        k_pos = base + t * TILE + lax.broadcasted_iota(jnp.int32, (TILE, TILE), 0)
        seen = (k_pos >= doc_start) & (k_pos <= q_pos)
        bias_ref[pl.ds(t * TILE, TILE), :] = jnp.where(seen, 0.0, NEG)
    for copy in copies:
        copy.wait()


def scores(qs_ref, dos_ref, kv_ref, bias_ref, at, part):
    dp = dot(kv_ref[:, HEAD:], dos_ref[part, :], NT)
    s = dot(kv_ref[:, :HEAD], qs_ref[part, :], NT) * (SCALE * LOG2E)
    s = s + twice(bias_ref[pl.ds(at * CHUNK, CHUNK), :])
    m = jnp.max(s, axis=0, keepdims=True)
    e = jnp.exp2(s - m)
    total = jnp.sum(e, axis=0, keepdims=True)
    return e, dp, m, total, jnp.sum(e * dp, axis=0, keepdims=True)


def parts_of(qs_ref):
    return [pl.ds(j * STEP, STEP) for j in range(qs_ref.shape[0] // STEP)]


def score_kernel(at, qs_ref, dos_ref, kv_ref, bias_ref, e_ref, dp_ref, stats_ref):
    for part in parts_of(qs_ref):
        e, dp, m, total, delta = scores(qs_ref, dos_ref, kv_ref, bias_ref, at, part)
        e_ref[:, part] = e
        dp_ref[:, part] = dp
        stats_ref[0:1, part] = m
        stats_ref[1:2, part] = total
        stats_ref[2:3, part] = delta


def grads(qs_ref, dos_ref, w_ref, ds_ref, out_ref):
    out_ref[:, :HEAD] = (dot(ds_ref[...], qs_ref[...], NN) * SCALE).astype(out_ref.dtype)
    out_ref[:, HEAD:] = dot(w_ref[...], dos_ref[...], NN).astype(out_ref.dtype)


def last_kernel(
    at, qs_ref, dos_ref, kv_ref, bias_ref, one_ref, two_ref,
    w_ref, ds_ref, stats_ref, out_ref,
):
    for part in parts_of(qs_ref):
        e, dp, m, total, delta = scores(qs_ref, dos_ref, kv_ref, bias_ref, at, part)
        m_one, m_two = one_ref[0:1, part], two_ref[0:1, part]
        top = jnp.maximum(m, jnp.maximum(m_one, m_two))
        a, a_one, a_two = (jnp.exp2(x - top) for x in (m, m_one, m_two))
        total = a * total + a_one * one_ref[1:2, part] + a_two * two_ref[1:2, part]
        delta = a * delta + a_one * one_ref[2:3, part] + a_two * two_ref[2:3, part]
        r = 1.0 / total
        delta = delta * r
        p = e * (a * r)
        w_ref[:, part] = p.astype(BF16)
        ds_ref[:, part] = (p * (dp - delta)).astype(BF16)
        stats_ref[0:1, part] = a_one * r
        stats_ref[1:2, part] = a_two * r
        stats_ref[2:3, part] = delta
    grads(qs_ref, dos_ref, w_ref, ds_ref, out_ref)


def grad_kernel(row, qs_ref, dos_ref, e_ref, dp_ref, stats_ref, w_ref, ds_ref, out_ref):
    for part in parts_of(qs_ref):
        p = e_ref[:, part] * stats_ref[row : row + 1, part]
        w_ref[:, part] = p.astype(BF16)
        ds_ref[:, part] = (p * (dp_ref[:, part] - stats_ref[2:3, part])).astype(BF16)
    grads(qs_ref, dos_ref, w_ref, ds_ref, out_ref)


def query_kernel(far_ref, mid_ref, near_ref, *refs):
    ws, dss, (o_ref, dq_ref, t_ref) = refs[:3], refs[3:6], refs[6:]
    for t, ref in enumerate((far_ref, mid_ref, near_ref)):
        t_ref[:, pl.ds(t * CHUNK, CHUNK)] = ref[...].T
    for j, part in enumerate(pl.ds(j * STEP, STEP) for j in range(ws[0].shape[1] // STEP)):
        w = jnp.concatenate([ref[:, part] for ref in ws], 0)
        ds = jnp.concatenate([ref[:, part] for ref in dss], 0)
        o = dot(t_ref[HEAD:, :], w, NN).astype(BF16)
        dq = (dot(t_ref[:HEAD, :], ds, NN) * SCALE).astype(BF16)
        for x, ref in ((o, o_ref), (dq, dq_ref)):
            ref[:, pl.ds(j * STEP, HEAD)] = x[:, :TILE].T
            ref[:, pl.ds(j * STEP + HEAD, HEAD)] = x[:, TILE:].T


def call(kernel, args, outs, flops=0, scratch=(), spaces=None, limit=16):
    vmem = pl.BlockSpec(memory_space=pltpu.VMEM)
    specs = [pl.BlockSpec(memory_space=s) for s in spaces or [pltpu.VMEM] * len(args)]
    outs = tuple(jax.ShapeDtypeStruct(shape, dtype) for shape, dtype in outs)
    size = sum(x.size * x.dtype.itemsize for x in list(args) + list(outs))
    return pl.pallas_call(
        kernel,
        out_shape=outs,
        in_specs=specs,
        out_specs=(vmem,) * len(outs),
        scratch_shapes=list(scratch),
        compiler_params=pltpu.CompilerParams(vmem_limit_bytes=limit << 20),
        cost_estimate=pl.CostEstimate(flops=flops, transcendentals=0, bytes_accessed=size),
    )(*args)


def prepare(lens, index, q, do):
    n = q.shape[0] * q.shape[1] // HEAD
    q, do = (pltpu.with_memory_space_constraint(x, pltpu.HBM) for x in (q, do))
    return call(
        stack_kernel, (lens, index, q, do),
        (((n, HEAD), BF16), ((n, HEAD), BF16), ((SPAN, TILE), F32)),
        spaces=[pltpu.SMEM, pltpu.SMEM, pltpu.HBM, pltpu.HBM],
        scratch=(pltpu.SemaphoreType.DMA((2, q.shape[1] // HEAD)),),
    )


def score_part(at, qs, dos, kv, bias):
    n = qs.shape[0]
    return call(
        functools.partial(score_kernel, at), (qs, dos, kv, bias),
        (((CHUNK, n), F32), ((CHUNK, n), F32), ((8, n), F32)), 4 * CHUNK * n * HEAD,
    )


def last_part(at, qs, dos, kv, bias, one, two):
    n = qs.shape[0]
    return call(
        functools.partial(last_kernel, at), (qs, dos, kv, bias, one, two),
        (((CHUNK, n), BF16), ((CHUNK, n), BF16), ((8, n), F32), ((CHUNK, 2 * HEAD), BF16)),
        8 * CHUNK * n * HEAD,
    )


def grad_part(row, qs, dos, e, dp, stats, dtype):
    n = qs.shape[0]
    return call(
        functools.partial(grad_kernel, row), (qs, dos, e, dp, stats),
        (((CHUNK, n), BF16), ((CHUNK, n), BF16), ((CHUNK, 2 * HEAD), dtype)),
        4 * CHUNK * n * HEAD,
    )


def query_part(kvs, ws, dss, shape):
    n = ws[0].shape[1]
    return call(
        query_kernel, (*kvs, *ws, *dss), ((shape, BF16), (shape, BF16)),
        4 * SPAN * n * HEAD, scratch=(pltpu.VMEM((2 * HEAD, SPAN), BF16),),
    )


def per_device(queries, keys, values, output_gradient, doc_lens):
    index = lax.axis_index(SEQ_AXES).astype(jnp.int32).reshape(1)
    own = jnp.concatenate([keys, values], 1)
    before = shifted(own, 1)
    qs, dos, bias = prepare(doc_lens, index, queries, output_gradient)
    before, bias = lax.optimization_barrier((before, bias))
    near = jnp.concatenate([before, own], 0)
    mid = shifted(near, 2)
    far = shifted(near, 4)
    e_near, dp_near, st_near = score_part(2, qs, dos, near, bias)
    e_mid, dp_mid, st_mid = score_part(1, qs, dos, mid, bias)
    w_far, ds_far, stats, g_far = last_part(0, qs, dos, far, bias, st_near, st_mid)
    from_far = shifted(g_far, -4)
    w_mid, ds_mid, g_mid = grad_part(1, qs, dos, e_mid, dp_mid, stats, BF16)
    from_mid = shifted(g_mid, -2)
    w_near, ds_near, g_near = grad_part(0, qs, dos, e_near, dp_near, stats, F32)
    summed = from_far.astype(F32) + from_mid.astype(F32) + g_near
    back = shifted(summed[:TILE].astype(BF16), -1).astype(F32)
    attended, query_grad = query_part(
        (far, mid, near), (w_far, w_mid, w_near), (ds_far, ds_mid, ds_near), queries.shape
    )
    total = (summed[TILE:] + back).astype(BF16)
    return attended, query_grad, total[:, :HEAD], total[:, HEAD:]


def bench(lens, index, q, do, far, mid, near):
    qs, dos, bias = prepare(lens, index, q, do)
    e_near, dp_near, st_near = score_part(2, qs, dos, near, bias)
    e_mid, dp_mid, st_mid = score_part(1, qs, dos, mid, bias)
    w_far, ds_far, stats, g_far = last_part(0, qs, dos, far, bias, st_near, st_mid)
    w_mid, ds_mid, g_mid = grad_part(1, qs, dos, e_mid, dp_mid, stats, BF16)
    w_near, ds_near, g_near = grad_part(0, qs, dos, e_near, dp_near, stats, F32)
    o, dq = query_part(
        (far, mid, near), (w_far, w_mid, w_near), (ds_far, ds_mid, ds_near), q.shape
    )
    return o, dq, jnp.concatenate([g_far.astype(F32), g_mid.astype(F32), g_near], 0)


def solution(mesh):
    rows = P(SEQ_AXES, "tp")
    return jax.shard_map(
        per_device,
        mesh=mesh,
        in_specs=(rows, rows, rows, rows, P()),
        out_specs=(rows, rows, rows, rows),
        check_vma=False,
    )
```

```python
import functools

import jax
import jax.numpy as jnp
from jax import lax
from jax.experimental import pallas as pl
from jax.experimental.pallas import tpu as pltpu
from jax.sharding import PartitionSpec as P

HEAD = 128
TILE = 128
REACH = 5
SPAN = (REACH + 1) * TILE
CHUNK = 2 * TILE
SEQ_AXES = ("dp", "ctx")
SCALE = HEAD ** (-0.5)
LOG2E = 1.4426950408889634
NEG = -1e30
STEP = 2 * TILE
KEY, VALUE = pl.ds(0, HEAD), pl.ds(HEAD, HEAD)

NT = (((1,), (1,)), ((), ()))
NN = (((1,), (0,)), ((), ()))
BF16 = jnp.bfloat16
F32 = jnp.float32


def dot(a, b, dims):
    return lax.dot_general(a, b, dims, preferred_element_type=F32)


def shifted(block, distance):
    devices = range(lax.axis_size(SEQ_AXES))
    route = [(i - distance, i) for i in devices if i - distance in devices]
    return lax.ppermute(block, SEQ_AXES, route)


def twice(x):
    return jnp.concatenate([x, x], 1)


def stack_kernel(
    lens_ref, index_ref, q_ref, do_ref, qs_ref, dos_ref, bias_ref, sems
):
    copies = []
    for h in range(q_ref.shape[1] // HEAD):
        part = pl.ds(h * HEAD, HEAD)
        for x, (src, dst) in enumerate(((q_ref, qs_ref), (do_ref, dos_ref))):
            copies.append(
                pltpu.make_async_copy(src.at[:, part], dst.at[part, :], sems.at[x, h])
            )
            copies[-1].start()
    base = (index_ref[0] - REACH) * TILE
    q_pos = base + REACH * TILE + lax.broadcasted_iota(jnp.int32, (8, TILE), 1)
    doc_start = jnp.zeros((8, TILE), jnp.int32)
    end = jnp.int32(0)
    for i in range(lens_ref.shape[0]):
        end = end + lens_ref[i]
        doc_start = jnp.where(q_pos >= end, jnp.maximum(doc_start, end), doc_start)
    q_pos, doc_start = q_pos[:1], doc_start[:1]
    for t in range(REACH + 1):
        k_pos = base + t * TILE + lax.broadcasted_iota(jnp.int32, (TILE, TILE), 0)
        seen = (k_pos >= doc_start) & (k_pos <= q_pos)
        bias_ref[pl.ds(t * TILE, TILE), :] = jnp.where(seen, 0.0, NEG)
    for copy in copies:
        copy.wait()


def scores(qs_ref, dos_ref, kv_ref, bias_ref, at, part):
    dp = dot(kv_ref[:, HEAD:], dos_ref[part, :], NT)
    s = dot(kv_ref[:, :HEAD], qs_ref[part, :], NT) * (SCALE * LOG2E)
    s = s + twice(bias_ref[pl.ds(at * CHUNK, CHUNK), :])
    m = jnp.max(s, axis=0, keepdims=True)
    e = jnp.exp2(s - m)
    total = jnp.sum(e, axis=0, keepdims=True)
    return e, dp, m, total, jnp.sum(e * dp, axis=0, keepdims=True)


def parts_of(qs_ref):
    return [pl.ds(j * STEP, STEP) for j in range(qs_ref.shape[0] // STEP)]


def score_kernel(at, qs_ref, dos_ref, kv_ref, bias_ref, e_ref, dp_ref, stats_ref):
    for part in parts_of(qs_ref):
        e, dp, m, total, delta = scores(qs_ref, dos_ref, kv_ref, bias_ref, at, part)
        e_ref[:, part] = e
        dp_ref[:, part] = dp
        stats_ref[0:1, part] = m
        stats_ref[1:2, part] = total
        stats_ref[2:3, part] = delta


def grads(qs_ref, dos_ref, w_ref, ds_ref, out_ref):
    out_ref[:, :HEAD] = (dot(ds_ref[...], qs_ref[...], NN) * SCALE).astype(out_ref.dtype)
    out_ref[:, HEAD:] = dot(w_ref[...], dos_ref[...], NN).astype(out_ref.dtype)


def last_kernel(
    at, qs_ref, dos_ref, kv_ref, bias_ref, one_ref, two_ref,
    w_ref, ds_ref, stats_ref, out_ref,
):
    for part in parts_of(qs_ref):
        e, dp, m, total, delta = scores(qs_ref, dos_ref, kv_ref, bias_ref, at, part)
        m_one, m_two = one_ref[0:1, part], two_ref[0:1, part]
        top = jnp.maximum(m, jnp.maximum(m_one, m_two))
        a, a_one, a_two = (jnp.exp2(x - top) for x in (m, m_one, m_two))
        total = a * total + a_one * one_ref[1:2, part] + a_two * two_ref[1:2, part]
        delta = a * delta + a_one * one_ref[2:3, part] + a_two * two_ref[2:3, part]
        r = 1.0 / total
        delta = delta * r
        p = e * (a * r)
        w_ref[:, part] = p.astype(BF16)
        ds_ref[:, part] = (p * (dp - delta)).astype(BF16)
        stats_ref[0:1, part] = a_one * r
        stats_ref[1:2, part] = a_two * r
        stats_ref[2:3, part] = delta
    grads(qs_ref, dos_ref, w_ref, ds_ref, out_ref)


def grad_kernel(row, qs_ref, dos_ref, e_ref, dp_ref, stats_ref, w_ref, ds_ref, out_ref):
    for part in parts_of(qs_ref):
        p = e_ref[:, part] * stats_ref[row : row + 1, part]
        w_ref[:, part] = p.astype(BF16)
        ds_ref[:, part] = (p * (dp_ref[:, part] - stats_ref[2:3, part])).astype(BF16)
    grads(qs_ref, dos_ref, w_ref, ds_ref, out_ref)


def query_kernel(far_ref, mid_ref, near_ref, *refs):
    ws, dss, (o_ref, dq_ref, t_ref) = refs[:3], refs[3:6], refs[6:]
    for t, ref in enumerate((far_ref, mid_ref, near_ref)):
        t_ref[:, pl.ds(t * CHUNK, CHUNK)] = ref[...].T
    for j, part in enumerate(pl.ds(j * STEP, STEP) for j in range(ws[0].shape[1] // STEP)):
        w = jnp.concatenate([ref[:, part] for ref in ws], 0)
        ds = jnp.concatenate([ref[:, part] for ref in dss], 0)
        o = dot(t_ref[HEAD:, :], w, NN).astype(BF16)
        dq = (dot(t_ref[:HEAD, :], ds, NN) * SCALE).astype(BF16)
        for x, ref in ((o, o_ref), (dq, dq_ref)):
            ref[:, pl.ds(j * STEP, HEAD)] = x[:, :TILE].T
            ref[:, pl.ds(j * STEP + HEAD, HEAD)] = x[:, TILE:].T


def call(kernel, args, outs, flops=0, scratch=(), spaces=None, limit=16):
    vmem = pl.BlockSpec(memory_space=pltpu.VMEM)
    specs = [pl.BlockSpec(memory_space=s) for s in spaces or [pltpu.VMEM] * len(args)]
    outs = tuple(jax.ShapeDtypeStruct(shape, dtype) for shape, dtype in outs)
    size = sum(x.size * x.dtype.itemsize for x in list(args) + list(outs))
    return pl.pallas_call(
        kernel,
        out_shape=outs,
        in_specs=specs,
        out_specs=(vmem,) * len(outs),
        scratch_shapes=list(scratch),
        compiler_params=pltpu.CompilerParams(vmem_limit_bytes=limit << 20),
        cost_estimate=pl.CostEstimate(flops=flops, transcendentals=0, bytes_accessed=size),
    )(*args)


def prepare(lens, index, q, do):
    n = q.shape[0] * q.shape[1] // HEAD
    q, do = (pltpu.with_memory_space_constraint(x, pltpu.HBM) for x in (q, do))
    return call(
        stack_kernel, (lens, index, q, do),
        (((n, HEAD), BF16), ((n, HEAD), BF16), ((SPAN, TILE), F32)),
        spaces=[pltpu.SMEM, pltpu.SMEM, pltpu.HBM, pltpu.HBM],
        scratch=(pltpu.SemaphoreType.DMA((2, q.shape[1] // HEAD)),),
    )


def join_kernel(k_ref, v_ref, out_ref, sems):
    copies = [
        pltpu.make_async_copy(k_ref, out_ref.at[:, KEY], sems.at[0]),
        pltpu.make_async_copy(v_ref, out_ref.at[:, VALUE], sems.at[1]),
    ]
    for copy in copies:
        copy.start()
    for copy in copies:
        copy.wait()


def join(k, v):
    k, v = (pltpu.with_memory_space_constraint(x, pltpu.HBM) for x in (k, v))
    return call(
        join_kernel, (k, v), (((k.shape[0], 2 * HEAD), BF16),), spaces=[pltpu.HBM] * 2,
        scratch=(pltpu.SemaphoreType.DMA((2,)),),
    )[0]


def score_part(at, qs, dos, kv, bias):
    n = qs.shape[0]
    return call(
        functools.partial(score_kernel, at), (qs, dos, kv, bias),
        (((CHUNK, n), F32), ((CHUNK, n), F32), ((8, n), F32)), 4 * CHUNK * n * HEAD,
    )


def last_part(at, qs, dos, kv, bias, one, two):
    n = qs.shape[0]
    return call(
        functools.partial(last_kernel, at), (qs, dos, kv, bias, one, two),
        (((CHUNK, n), BF16), ((CHUNK, n), BF16), ((8, n), F32), ((CHUNK, 2 * HEAD), BF16)),
        8 * CHUNK * n * HEAD,
    )


def grad_part(row, qs, dos, e, dp, stats, dtype):
    n = qs.shape[0]
    return call(
        functools.partial(grad_kernel, row), (qs, dos, e, dp, stats),
        (((CHUNK, n), BF16), ((CHUNK, n), BF16), ((CHUNK, 2 * HEAD), dtype)),
        4 * CHUNK * n * HEAD,
    )


def query_part(kvs, ws, dss, shape):
    n = ws[0].shape[1]
    return call(
        query_kernel, (*kvs, *ws, *dss), ((shape, BF16), (shape, BF16)),
        4 * SPAN * n * HEAD, scratch=(pltpu.VMEM((2 * HEAD, SPAN), BF16),),
    )


def per_device(queries, keys, values, output_gradient, doc_lens):
    index = lax.axis_index(SEQ_AXES).astype(jnp.int32).reshape(1)
    own = join(keys, values)
    before = shifted(own, 1)
    qs, dos, bias = prepare(doc_lens, index, queries, output_gradient)
    before, bias = lax.optimization_barrier((before, bias))
    near = jnp.concatenate([before, own], 0)
    mid = shifted(near, 2)
    far = shifted(near, 4)
    e_near, dp_near, st_near = score_part(2, qs, dos, near, bias)
    e_far, dp_far, st_far = score_part(0, qs, dos, far, bias)
    w_mid, ds_mid, stats, g_mid = last_part(1, qs, dos, mid, bias, st_near, st_far)
    from_mid = shifted(g_mid, -2)
    w_far, ds_far, g_far = grad_part(1, qs, dos, e_far, dp_far, stats, BF16)
    from_far = shifted(g_far, -4)
    w_near, ds_near, g_near = grad_part(0, qs, dos, e_near, dp_near, stats, F32)
    attended, query_grad = query_part(
        (far, mid, near), (w_far, w_mid, w_near), (ds_far, ds_mid, ds_near), queries.shape
    )
    attended, query_grad, from_far, from_mid = lax.optimization_barrier(
        (attended, query_grad, from_far, from_mid)
    )
    summed = from_far.astype(F32) + from_mid.astype(F32) + g_near
    back = shifted(summed[:TILE].astype(BF16), -1).astype(F32)
    total = (summed[TILE:] + back).astype(BF16)
    return attended, query_grad, total[:, :HEAD], total[:, HEAD:]


def solution(mesh):
    rows = P(SEQ_AXES, "tp")
    return jax.shard_map(
        per_device,
        mesh=mesh,
        in_specs=(rows, rows, rows, rows, P()),
        out_specs=(rows, rows, rows, rows),
        check_vma=False,
    )
```

```python
import functools

import jax
import jax.numpy as jnp
from jax import lax
from jax.experimental import pallas as pl
from jax.experimental.pallas import tpu as pltpu
from jax.sharding import PartitionSpec as P

HEAD = 128
TILE = 128
REACH = 5
SPAN = (REACH + 1) * TILE
CHUNK = 2 * TILE
SEQ_AXES = ("dp", "ctx")
SCALE = HEAD ** (-0.5)
LOG2E = 1.4426950408889634
NEG = -1e30
STEP = 2 * TILE
PIECES = 4
KEY, VALUE = pl.ds(0, HEAD), pl.ds(HEAD, HEAD)

NT = (((1,), (1,)), ((), ()))
NN = (((1,), (0,)), ((), ()))
BF16 = jnp.bfloat16
F32 = jnp.float32


def dot(a, b, dims):
    return lax.dot_general(a, b, dims, preferred_element_type=F32)


def shifted(block, distance):
    devices = range(lax.axis_size(SEQ_AXES))
    route = [(i - distance, i) for i in devices if i - distance in devices]
    return lax.ppermute(block, SEQ_AXES, route)


def twice(x):
    return jnp.concatenate([x, x], 1)


def prepare_kernel(
    lens_hbm, index_ref, q_hbm, do_hbm, q_ref, do_ref, bias_ref, lens_ref, sems, lens_sem
):
    lens = pltpu.make_async_copy(lens_hbm, lens_ref, lens_sem)
    lens.start()
    copies = []
    for c in range(PIECES):
        rows = pl.ds(c * (TILE // PIECES), TILE // PIECES)
        for x, (src, dst) in enumerate(((q_hbm, q_ref), (do_hbm, do_ref))):
            copies.append(
                pltpu.make_async_copy(src.at[rows, :], dst.at[rows, :], sems.at[x, c])
            )
            copies[-1].start()
    lens.wait()
    base = (index_ref[0] - REACH) * TILE
    q_pos = base + REACH * TILE + lax.broadcasted_iota(jnp.int32, (8, TILE), 1)
    doc_start = jnp.zeros((8, TILE), jnp.int32)
    end = jnp.int32(0)
    for i in range(lens_ref.shape[0]):
        end = end + lens_ref[i]
        doc_start = jnp.where(q_pos >= end, jnp.maximum(doc_start, end), doc_start)
    q_pos, doc_start = q_pos[:1], doc_start[:1]
    for t in range(REACH + 1):
        k_pos = base + t * TILE + lax.broadcasted_iota(jnp.int32, (TILE, TILE), 0)
        seen = (k_pos >= doc_start) & (k_pos <= q_pos)
        bias_ref[pl.ds(t * TILE, TILE), :] = jnp.where(seen, 0.0, NEG)
    for copy in copies:
        copy.wait()


def stacked(ref, heads):
    return jnp.concatenate([ref[:, pl.ds(h * HEAD, HEAD)] for h in heads], 0)


def scores(qs_ref, dos_ref, kv_ref, bias_ref, at, part):
    heads = (part.start // HEAD, part.start // HEAD + 1)
    dp = dot(kv_ref[:, HEAD:], stacked(dos_ref, heads), NT)
    s = dot(kv_ref[:, :HEAD], stacked(qs_ref, heads), NT) * (SCALE * LOG2E)
    s = s + twice(bias_ref[pl.ds(at * CHUNK, CHUNK), :])
    m = jnp.max(s, axis=0, keepdims=True)
    e = jnp.exp2(s - m)
    total = jnp.sum(e, axis=0, keepdims=True)
    return e, dp, m, total, jnp.sum(e * dp, axis=0, keepdims=True)


def parts_of(qs_ref):
    return [pl.ds(j * STEP, STEP) for j in range(qs_ref.shape[1] // STEP)]


def score_kernel(at, qs_ref, dos_ref, kv_ref, bias_ref, e_ref, dp_ref, stats_ref):
    for part in parts_of(qs_ref):
        e, dp, m, total, delta = scores(qs_ref, dos_ref, kv_ref, bias_ref, at, part)
        e_ref[:, part] = e
        dp_ref[:, part] = dp
        stats_ref[0:1, part] = m
        stats_ref[1:2, part] = total
        stats_ref[2:3, part] = delta


def grads(qs_ref, dos_ref, w_ref, ds_ref, out_ref):
    heads = range(qs_ref.shape[1] // HEAD)
    out_ref[:, :HEAD] = (dot(ds_ref[...], stacked(qs_ref, heads), NN) * SCALE).astype(out_ref.dtype)
    out_ref[:, HEAD:] = dot(w_ref[...], stacked(dos_ref, heads), NN).astype(out_ref.dtype)


def last_kernel(
    at, qs_ref, dos_ref, kv_ref, bias_ref, one_ref, two_ref, e_ref, dp_ref, stats_ref
):
    for part in parts_of(qs_ref):
        e, dp, m, total, delta = scores(qs_ref, dos_ref, kv_ref, bias_ref, at, part)
        e_ref[:, part] = e
        dp_ref[:, part] = dp
        m_one, m_two = one_ref[0:1, part], two_ref[0:1, part]
        top = jnp.maximum(m, jnp.maximum(m_one, m_two))
        a, a_one, a_two = (jnp.exp2(x - top) for x in (m, m_one, m_two))
        total = a * total + a_one * one_ref[1:2, part] + a_two * two_ref[1:2, part]
        delta = a * delta + a_one * one_ref[2:3, part] + a_two * two_ref[2:3, part]
        r = 1.0 / total
        stats_ref[0:1, part] = a_one * r
        stats_ref[1:2, part] = a_two * r
        stats_ref[2:3, part] = a * r
        stats_ref[3:4, part] = delta * r


def grad_kernel(row, qs_ref, dos_ref, e_ref, dp_ref, stats_ref, w_ref, ds_ref, out_ref):
    for part in parts_of(qs_ref):
        p = e_ref[:, part] * stats_ref[row : row + 1, part]
        w_ref[:, part] = p.astype(BF16)
        ds_ref[:, part] = (p * (dp_ref[:, part] - stats_ref[3:4, part])).astype(BF16)
    grads(qs_ref, dos_ref, w_ref, ds_ref, out_ref)


def query_kernel(far_ref, mid_ref, near_ref, *refs):
    ws, dss, (o_ref, dq_ref, t_ref) = refs[:3], refs[3:6], refs[6:]
    for t, ref in enumerate((far_ref, mid_ref, near_ref)):
        t_ref[:, pl.ds(t * CHUNK, CHUNK)] = ref[...].T
    for j, part in enumerate(pl.ds(j * STEP, STEP) for j in range(ws[0].shape[1] // STEP)):
        w = jnp.concatenate([ref[:, part] for ref in ws], 0)
        ds = jnp.concatenate([ref[:, part] for ref in dss], 0)
        o = dot(t_ref[HEAD:, :], w, NN).astype(BF16)
        dq = (dot(t_ref[:HEAD, :], ds, NN) * SCALE).astype(BF16)
        for x, ref in ((o, o_ref), (dq, dq_ref)):
            ref[:, pl.ds(j * STEP, HEAD)] = x[:, :TILE].T
            ref[:, pl.ds(j * STEP + HEAD, HEAD)] = x[:, TILE:].T


def call(kernel, args, outs, flops=0, scratch=(), spaces=None, limit=16):
    vmem = pl.BlockSpec(memory_space=pltpu.VMEM)
    specs = [pl.BlockSpec(memory_space=s) for s in spaces or [pltpu.VMEM] * len(args)]
    outs = tuple(jax.ShapeDtypeStruct(shape, dtype) for shape, dtype in outs)
    size = sum(x.size * x.dtype.itemsize for x in list(args) + list(outs))
    return pl.pallas_call(
        kernel,
        out_shape=outs,
        in_specs=specs,
        out_specs=(vmem,) * len(outs),
        scratch_shapes=list(scratch),
        compiler_params=pltpu.CompilerParams(vmem_limit_bytes=limit << 20),
        cost_estimate=pl.CostEstimate(flops=flops, transcendentals=0, bytes_accessed=size),
    )(*args)


def in_hbm(*arrays):
    return [pltpu.with_memory_space_constraint(x, pltpu.HBM) for x in arrays]


def prepare(lens, index, q, do):
    lens, q, do = in_hbm(lens, q, do)
    return call(
        prepare_kernel, (lens, index, q, do),
        ((q.shape, BF16), (do.shape, BF16), ((SPAN, TILE), F32)),
        spaces=[pltpu.HBM, pltpu.SMEM, pltpu.HBM, pltpu.HBM],
        scratch=(
            pltpu.SMEM(lens.shape, jnp.int32),
            pltpu.SemaphoreType.DMA((2, PIECES)),
            pltpu.SemaphoreType.DMA,
        ),
    )


def join_kernel(k_ref, v_ref, out_ref, sems):
    copies = [
        pltpu.make_async_copy(k_ref, out_ref.at[:, KEY], sems.at[0]),
        pltpu.make_async_copy(v_ref, out_ref.at[:, VALUE], sems.at[1]),
    ]
    for copy in copies:
        copy.start()
    for copy in copies:
        copy.wait()


def join(k, v):
    k, v = in_hbm(k, v)
    return call(
        join_kernel, (k, v), (((k.shape[0], 2 * HEAD), BF16),), spaces=[pltpu.HBM] * 2,
        scratch=(pltpu.SemaphoreType.DMA((2,)),),
    )[0]


def score_part(at, qs, dos, kv, bias):
    n = qs.size // HEAD
    return call(
        functools.partial(score_kernel, at), (qs, dos, kv, bias),
        (((CHUNK, n), F32), ((CHUNK, n), F32), ((8, n), F32)), 4 * CHUNK * n * HEAD,
    )


def last_part(at, qs, dos, kv, bias, one, two):
    n = qs.size // HEAD
    return call(
        functools.partial(last_kernel, at), (qs, dos, kv, bias, one, two),
        (((CHUNK, n), F32), ((CHUNK, n), F32), ((8, n), F32)), 4 * CHUNK * n * HEAD,
    )


def grad_part(row, qs, dos, e, dp, stats, dtype):
    n = qs.size // HEAD
    return call(
        functools.partial(grad_kernel, row), (qs, dos, e, dp, stats),
        (((CHUNK, n), BF16), ((CHUNK, n), BF16), ((CHUNK, 2 * HEAD), dtype)),
        4 * CHUNK * n * HEAD,
    )


def query_part(kvs, ws, dss, shape):
    n = ws[0].shape[1]
    return call(
        query_kernel, (*kvs, *ws, *dss), ((shape, BF16), (shape, BF16)),
        4 * SPAN * n * HEAD, scratch=(pltpu.VMEM((2 * HEAD, SPAN), BF16),),
    )


def per_device(queries, keys, values, output_gradient, doc_lens):
    index = lax.axis_index(SEQ_AXES).astype(jnp.int32).reshape(1)
    own = join(keys, values)
    before = shifted(own, 1)
    qs, dos, bias = prepare(doc_lens, index, queries, output_gradient)
    before, bias = lax.optimization_barrier((before, bias))
    near = jnp.concatenate([before, own], 0)
    mid = shifted(near, 2)
    far = shifted(near, 4)
    e_near, dp_near, st_near = score_part(2, qs, dos, near, bias)
    e_far, dp_far, st_far = score_part(0, qs, dos, far, bias)
    e_mid, dp_mid, stats = last_part(1, qs, dos, mid, bias, st_near, st_far)
    w_mid, ds_mid, g_mid = grad_part(2, qs, dos, e_mid, dp_mid, stats, BF16)
    from_mid = shifted(g_mid, -2)
    w_far, ds_far, g_far = grad_part(1, qs, dos, e_far, dp_far, stats, BF16)
    from_far = shifted(g_far, -4)
    w_near, ds_near, g_near = grad_part(0, qs, dos, e_near, dp_near, stats, F32)
    attended, query_grad = query_part(
        (far, mid, near), (w_far, w_mid, w_near), (ds_far, ds_mid, ds_near), queries.shape
    )
    attended, query_grad, from_far, from_mid = lax.optimization_barrier(
        (attended, query_grad, from_far, from_mid)
    )
    summed = from_far.astype(F32) + from_mid.astype(F32) + g_near
    back = shifted(summed[:TILE].astype(BF16), -1).astype(F32)
    total = (summed[TILE:] + back).astype(BF16)
    return attended, query_grad, total[:, :HEAD], total[:, HEAD:]


def solution(mesh):
    rows = P(SEQ_AXES, "tp")
    return jax.shard_map(
        per_device,
        mesh=mesh,
        in_specs=(rows, rows, rows, rows, P()),
        out_specs=(rows, rows, rows, rows),
        check_vma=False,
    )
```

```python
import functools

import jax
import jax.numpy as jnp
from jax import lax
from jax.experimental import pallas as pl
from jax.experimental.pallas import tpu as pltpu
from jax.sharding import PartitionSpec as P

HEAD = 128
TILE = 128
REACH = 5
SPAN = (REACH + 1) * TILE
CHUNK = 2 * TILE
SEQ_AXES = ("dp", "ctx")
SCALE = HEAD ** (-0.5)
LOG2E = 1.4426950408889634
NEG = -1e30
STEP = 2 * TILE
PIECES = 4
KEY, VALUE = pl.ds(0, HEAD), pl.ds(HEAD, HEAD)

NT = (((1,), (1,)), ((), ()))
NN = (((1,), (0,)), ((), ()))
BF16 = jnp.bfloat16
F32 = jnp.float32


def dot(a, b, dims):
    return lax.dot_general(a, b, dims, preferred_element_type=F32)


def shifted(block, distance):
    devices = range(lax.axis_size(SEQ_AXES))
    route = [(i - distance, i) for i in devices if i - distance in devices]
    return lax.ppermute(block, SEQ_AXES, route)


def twice(x):
    return jnp.concatenate([x, x], 1)


def prepare_kernel(
    lens_hbm, index_ref, q_hbm, do_hbm, q_ref, do_ref, bias_ref, lens_ref, sems, lens_sem
):
    lens = pltpu.make_async_copy(lens_hbm, lens_ref, lens_sem)
    lens.start()
    copies = []
    for c in range(PIECES):
        rows = pl.ds(c * (TILE // PIECES), TILE // PIECES)
        for x, (src, dst) in enumerate(((q_hbm, q_ref), (do_hbm, do_ref))):
            copies.append(
                pltpu.make_async_copy(src.at[rows, :], dst.at[rows, :], sems.at[x, c])
            )
            copies[-1].start()
    lens.wait()
    base = (index_ref[0] - REACH) * TILE
    q_pos = base + REACH * TILE + lax.broadcasted_iota(jnp.int32, (8, TILE), 1)
    doc_start = jnp.zeros((8, TILE), jnp.int32)
    end = jnp.int32(0)
    for i in range(lens_ref.shape[0]):
        end = end + lens_ref[i]
        doc_start = jnp.where(q_pos >= end, jnp.maximum(doc_start, end), doc_start)
    q_pos, doc_start = q_pos[:1], doc_start[:1]
    for t in range(REACH + 1):
        k_pos = base + t * TILE + lax.broadcasted_iota(jnp.int32, (TILE, TILE), 0)
        seen = (k_pos >= doc_start) & (k_pos <= q_pos)
        bias_ref[pl.ds(t * TILE, TILE), :] = jnp.where(seen, 0.0, NEG)
    for copy in copies:
        copy.wait()


def stacked(ref, heads):
    return jnp.concatenate([ref[:, pl.ds(h * HEAD, HEAD)] for h in heads], 0)


def scores(qs_ref, dos_ref, kv_ref, bias_ref, at, part):
    heads = (part.start // HEAD, part.start // HEAD + 1)
    dp = dot(kv_ref[:, HEAD:], stacked(dos_ref, heads), NT)
    s = dot(kv_ref[:, :HEAD], stacked(qs_ref, heads), NT) * (SCALE * LOG2E)
    s = s + twice(bias_ref[pl.ds(at * CHUNK, CHUNK), :])
    m = jnp.max(s, axis=0, keepdims=True)
    e = jnp.exp2(s - m)
    total = jnp.sum(e, axis=0, keepdims=True)
    return e, dp, m, total, jnp.sum(e * dp, axis=0, keepdims=True)


def parts_of(qs_ref):
    return [pl.ds(j * STEP, STEP) for j in range(qs_ref.shape[1] // STEP)]


def score_kernel(at, qs_ref, dos_ref, kv_ref, bias_ref, e_ref, dp_ref, stats_ref):
    for part in parts_of(qs_ref):
        e, dp, m, total, delta = scores(qs_ref, dos_ref, kv_ref, bias_ref, at, part)
        e_ref[:, part] = e
        dp_ref[:, part] = dp
        stats_ref[0:1, part] = m
        stats_ref[1:2, part] = total
        stats_ref[2:3, part] = delta


def grads(qs_ref, dos_ref, w_ref, ds_ref, out_ref):
    heads = range(qs_ref.shape[1] // HEAD)
    out_ref[:, :HEAD] = (dot(ds_ref[...], stacked(qs_ref, heads), NN) * SCALE).astype(out_ref.dtype)
    out_ref[:, HEAD:] = dot(w_ref[...], stacked(dos_ref, heads), NN).astype(out_ref.dtype)


def last_kernel(
    at, qs_ref, dos_ref, kv_ref, bias_ref, one_ref, two_ref, e_ref, dp_ref, stats_ref
):
    for part in parts_of(qs_ref):
        e, dp, m, total, delta = scores(qs_ref, dos_ref, kv_ref, bias_ref, at, part)
        e_ref[:, part] = e
        dp_ref[:, part] = dp
        m_one, m_two = one_ref[0:1, part], two_ref[0:1, part]
        top = jnp.maximum(m, jnp.maximum(m_one, m_two))
        a, a_one, a_two = (jnp.exp2(x - top) for x in (m, m_one, m_two))
        total = a * total + a_one * one_ref[1:2, part] + a_two * two_ref[1:2, part]
        delta = a * delta + a_one * one_ref[2:3, part] + a_two * two_ref[2:3, part]
        r = 1.0 / total
        stats_ref[0:1, part] = a_one * r
        stats_ref[1:2, part] = a_two * r
        stats_ref[2:3, part] = a * r
        stats_ref[3:4, part] = delta * r


def grad_kernel(row, qs_ref, dos_ref, e_ref, dp_ref, stats_ref, w_ref, ds_ref, out_ref):
    for part in parts_of(qs_ref):
        p = e_ref[:, part] * stats_ref[row : row + 1, part]
        w_ref[:, part] = p.astype(BF16)
        ds_ref[:, part] = (p * (dp_ref[:, part] - stats_ref[3:4, part])).astype(BF16)
    grads(qs_ref, dos_ref, w_ref, ds_ref, out_ref)


def query_kernel(far_ref, mid_ref, near_ref, *refs):
    ws, dss, (o_ref, dq_ref, t_ref) = refs[:3], refs[3:6], refs[6:]
    for t, ref in enumerate((far_ref, mid_ref, near_ref)):
        t_ref[:, pl.ds(t * CHUNK, CHUNK)] = ref[...].T
    for j, part in enumerate(pl.ds(j * STEP, STEP) for j in range(ws[0].shape[1] // STEP)):
        w = jnp.concatenate([ref[:, part] for ref in ws], 0)
        ds = jnp.concatenate([ref[:, part] for ref in dss], 0)
        o = dot(t_ref[HEAD:, :], w, NN).astype(BF16)
        dq = (dot(t_ref[:HEAD, :], ds, NN) * SCALE).astype(BF16)
        for x, ref in ((o, o_ref), (dq, dq_ref)):
            ref[:, pl.ds(j * STEP, HEAD)] = x[:, :TILE].T
            ref[:, pl.ds(j * STEP + HEAD, HEAD)] = x[:, TILE:].T


def call(kernel, args, outs, flops=0, scratch=(), spaces=None, limit=16):
    vmem = pl.BlockSpec(memory_space=pltpu.VMEM)
    specs = [pl.BlockSpec(memory_space=s) for s in spaces or [pltpu.VMEM] * len(args)]
    outs = tuple(jax.ShapeDtypeStruct(shape, dtype) for shape, dtype in outs)
    size = sum(x.size * x.dtype.itemsize for x in list(args) + list(outs))
    return pl.pallas_call(
        kernel,
        out_shape=outs,
        in_specs=specs,
        out_specs=(vmem,) * len(outs),
        scratch_shapes=list(scratch),
        compiler_params=pltpu.CompilerParams(vmem_limit_bytes=limit << 20),
        cost_estimate=pl.CostEstimate(flops=flops, transcendentals=0, bytes_accessed=size),
    )(*args)


def in_hbm(*arrays):
    return [pltpu.with_memory_space_constraint(x, pltpu.HBM) for x in arrays]


def prepare(lens, index, q, do):
    lens, q, do = in_hbm(lens, q, do)
    return call(
        prepare_kernel, (lens, index, q, do),
        ((q.shape, BF16), (do.shape, BF16), ((SPAN, TILE), F32)),
        spaces=[pltpu.HBM, pltpu.SMEM, pltpu.HBM, pltpu.HBM],
        scratch=(
            pltpu.SMEM(lens.shape, jnp.int32),
            pltpu.SemaphoreType.DMA((2, PIECES)),
            pltpu.SemaphoreType.DMA,
        ),
    )


def join_kernel(k_ref, v_ref, out_ref, sems):
    copies = [
        pltpu.make_async_copy(k_ref, out_ref.at[:, KEY], sems.at[0]),
        pltpu.make_async_copy(v_ref, out_ref.at[:, VALUE], sems.at[1]),
    ]
    for copy in copies:
        copy.start()
    for copy in copies:
        copy.wait()


def join(k, v):
    k, v = in_hbm(k, v)
    return call(
        join_kernel, (k, v), (((k.shape[0], 2 * HEAD), BF16),), spaces=[pltpu.HBM] * 2,
        scratch=(pltpu.SemaphoreType.DMA((2,)),),
    )[0]


def score_part(at, qs, dos, kv, bias):
    n = qs.size // HEAD
    return call(
        functools.partial(score_kernel, at), (qs, dos, kv, bias),
        (((CHUNK, n), F32), ((CHUNK, n), F32), ((8, n), F32)), 4 * CHUNK * n * HEAD,
    )


def last_part(at, qs, dos, kv, bias, one, two):
    n = qs.size // HEAD
    return call(
        functools.partial(last_kernel, at), (qs, dos, kv, bias, one, two),
        (((CHUNK, n), F32), ((CHUNK, n), F32), ((8, n), F32)), 4 * CHUNK * n * HEAD,
    )


def grad_part(row, qs, dos, e, dp, stats, dtype):
    n = qs.size // HEAD
    return call(
        functools.partial(grad_kernel, row), (qs, dos, e, dp, stats),
        (((CHUNK, n), BF16), ((CHUNK, n), BF16), ((CHUNK, 2 * HEAD), dtype)),
        4 * CHUNK * n * HEAD,
    )


def query_part(kvs, ws, dss, shape):
    n = ws[0].shape[1]
    return call(
        query_kernel, (*kvs, *ws, *dss), ((shape, BF16), (shape, BF16)),
        4 * SPAN * n * HEAD, scratch=(pltpu.VMEM((2 * HEAD, SPAN), BF16),),
    )


def per_device(queries, keys, values, output_gradient, doc_lens):
    index = lax.axis_index(SEQ_AXES).astype(jnp.int32).reshape(1)
    own = join(keys, values)
    before = shifted(own, 1)
    qs, dos, bias = prepare(doc_lens, index, queries, output_gradient)
    near = jnp.concatenate([before, own], 0)
    mid = shifted(near, 2)
    far = shifted(near, 4)
    e_near, dp_near, st_near = score_part(2, qs, dos, near, bias)
    e_far, dp_far, st_far = score_part(0, qs, dos, far, bias)
    e_mid, dp_mid, stats = last_part(1, qs, dos, mid, bias, st_near, st_far)
    w_mid, ds_mid, g_mid = grad_part(2, qs, dos, e_mid, dp_mid, stats, BF16)
    from_mid = shifted(g_mid, -2)
    w_far, ds_far, g_far = grad_part(1, qs, dos, e_far, dp_far, stats, BF16)
    from_far = shifted(g_far, -4)
    w_near, ds_near, g_near = grad_part(0, qs, dos, e_near, dp_near, stats, F32)
    attended, query_grad = query_part(
        (far, mid, near), (w_far, w_mid, w_near), (ds_far, ds_mid, ds_near), queries.shape
    )
    attended, query_grad, from_far, from_mid = lax.optimization_barrier(
        (attended, query_grad, from_far, from_mid)
    )
    summed = from_far.astype(F32) + from_mid.astype(F32) + g_near
    back = shifted(summed[:TILE].astype(BF16), -1).astype(F32)
    total = (summed[TILE:] + back).astype(BF16)
    return attended, query_grad, total[:, :HEAD], total[:, HEAD:]


def solution(mesh):
    rows = P(SEQ_AXES, "tp")
    return jax.shard_map(
        per_device,
        mesh=mesh,
        in_specs=(rows, rows, rows, rows, P()),
        out_specs=(rows, rows, rows, rows),
        check_vma=False,
    )
```

```python
import functools

import jax
import jax.numpy as jnp
from jax import lax
from jax.experimental import pallas as pl
from jax.experimental.pallas import tpu as pltpu
from jax.sharding import PartitionSpec as P

HEAD = 128
TILE = 128
REACH = 5
SPAN = (REACH + 1) * TILE
CHUNK = 2 * TILE
SEQ_AXES = ("dp", "ctx")
SCALE = HEAD ** (-0.5)
LOG2E = 1.4426950408889634
NEG = -1e30
STEP = 2 * TILE
PIECES = 4
KEY, VALUE = pl.ds(0, HEAD), pl.ds(HEAD, HEAD)

NT = (((1,), (1,)), ((), ()))
NN = (((1,), (0,)), ((), ()))
BF16 = jnp.bfloat16
F32 = jnp.float32


def dot(a, b, dims):
    return lax.dot_general(a, b, dims, preferred_element_type=F32)


def shifted(block, distance):
    devices = range(lax.axis_size(SEQ_AXES))
    route = [(i - distance, i) for i in devices if i - distance in devices]
    return lax.ppermute(block, SEQ_AXES, route)


def twice(x):
    return jnp.concatenate([x, x], 1)


def prepare_kernel(
    lens_hbm, index_ref, q_hbm, do_hbm, q_ref, do_ref, bias_ref, lens_ref, sems, lens_sem
):
    lens = pltpu.make_async_copy(lens_hbm, lens_ref, lens_sem)
    lens.start()
    copies = []
    for c in range(PIECES):
        rows = pl.ds(c * (TILE // PIECES), TILE // PIECES)
        for x, (src, dst) in enumerate(((q_hbm, q_ref), (do_hbm, do_ref))):
            copies.append(
                pltpu.make_async_copy(src.at[rows, :], dst.at[rows, :], sems.at[x, c])
            )
            copies[-1].start()
    lens.wait()
    base = (index_ref[0] - REACH) * TILE
    q_pos = base + REACH * TILE + lax.broadcasted_iota(jnp.int32, (8, TILE), 1)
    doc_start = jnp.zeros((8, TILE), jnp.int32)
    end = jnp.int32(0)
    for i in range(lens_ref.shape[0]):
        end = end + lens_ref[i]
        doc_start = jnp.where(q_pos >= end, jnp.maximum(doc_start, end), doc_start)
    q_pos, doc_start = q_pos[:1], doc_start[:1]
    for t in range(REACH + 1):
        k_pos = base + t * TILE + lax.broadcasted_iota(jnp.int32, (TILE, TILE), 0)
        seen = (k_pos >= doc_start) & (k_pos <= q_pos)
        bias_ref[pl.ds(t * TILE, TILE), :] = jnp.where(seen, 0.0, NEG)
    for copy in copies:
        copy.wait()


def stacked(ref, heads):
    return jnp.concatenate([ref[:, pl.ds(h * HEAD, HEAD)] for h in heads], 0)


def scores(qs_ref, dos_ref, kv_ref, bias_ref, at, part):
    heads = (part.start // HEAD, part.start // HEAD + 1)
    dp = dot(kv_ref[:, HEAD:], stacked(dos_ref, heads), NT)
    s = dot(kv_ref[:, :HEAD], stacked(qs_ref, heads), NT) * (SCALE * LOG2E)
    s = s + twice(bias_ref[pl.ds(at * CHUNK, CHUNK), :])
    m = jnp.max(s, axis=0, keepdims=True)
    e = jnp.exp2(s - m)
    total = jnp.sum(e, axis=0, keepdims=True)
    return e, dp, m, total, jnp.sum(e * dp, axis=0, keepdims=True)


def parts_of(qs_ref):
    return [pl.ds(j * STEP, STEP) for j in range(qs_ref.shape[1] // STEP)]


def score_kernel(at, qs_ref, dos_ref, kv_ref, bias_ref, e_ref, dp_ref, stats_ref):
    for part in parts_of(qs_ref):
        e, dp, m, total, delta = scores(qs_ref, dos_ref, kv_ref, bias_ref, at, part)
        e_ref[:, part] = e
        dp_ref[:, part] = dp
        stats_ref[0:1, part] = m
        stats_ref[1:2, part] = total
        stats_ref[2:3, part] = delta


def grads(qs_ref, dos_ref, w_ref, ds_ref, out_ref):
    heads = range(qs_ref.shape[1] // HEAD)
    out_ref[:, :HEAD] = (dot(ds_ref[...], stacked(qs_ref, heads), NN) * SCALE).astype(out_ref.dtype)
    out_ref[:, HEAD:] = dot(w_ref[...], stacked(dos_ref, heads), NN).astype(out_ref.dtype)


def last_kernel(
    at, qs_ref, dos_ref, kv_ref, bias_ref, one_ref, two_ref, e_ref, dp_ref, stats_ref
):
    for part in parts_of(qs_ref):
        e, dp, m, total, delta = scores(qs_ref, dos_ref, kv_ref, bias_ref, at, part)
        e_ref[:, part] = e
        dp_ref[:, part] = dp
        m_one, m_two = one_ref[0:1, part], two_ref[0:1, part]
        top = jnp.maximum(m, jnp.maximum(m_one, m_two))
        a, a_one, a_two = (jnp.exp2(x - top) for x in (m, m_one, m_two))
        total = a * total + a_one * one_ref[1:2, part] + a_two * two_ref[1:2, part]
        delta = a * delta + a_one * one_ref[2:3, part] + a_two * two_ref[2:3, part]
        r = 1.0 / total
        stats_ref[0:1, part] = a_one * r
        stats_ref[1:2, part] = a_two * r
        stats_ref[2:3, part] = a * r
        stats_ref[3:4, part] = delta * r


def grad_kernel(row, qs_ref, dos_ref, e_ref, dp_ref, stats_ref, w_ref, ds_ref, out_ref):
    for part in parts_of(qs_ref):
        p = e_ref[:, part] * stats_ref[row : row + 1, part]
        w_ref[:, part] = p.astype(BF16)
        ds_ref[:, part] = (p * (dp_ref[:, part] - stats_ref[3:4, part])).astype(BF16)
    grads(qs_ref, dos_ref, w_ref, ds_ref, out_ref)


def query_kernel(side, scale, far_ref, mid_ref, near_ref, *refs):
    ws, (out_ref, t_ref) = refs[:3], refs[3:]
    for t, ref in enumerate((far_ref, mid_ref, near_ref)):
        t_ref[:, pl.ds(t * CHUNK, CHUNK)] = ref[:, side].T
    for j, part in enumerate(pl.ds(j * STEP, STEP) for j in range(ws[0].shape[1] // STEP)):
        w = jnp.concatenate([ref[:, part] for ref in ws], 0)
        x = (dot(t_ref[...], w, NN) * scale).astype(BF16)
        out_ref[:, pl.ds(j * STEP, HEAD)] = x[:, :TILE].T
        out_ref[:, pl.ds(j * STEP + HEAD, HEAD)] = x[:, TILE:].T


def call(kernel, args, outs, flops=0, scratch=(), spaces=None, limit=16):
    vmem = pl.BlockSpec(memory_space=pltpu.VMEM)
    specs = [pl.BlockSpec(memory_space=s) for s in spaces or [pltpu.VMEM] * len(args)]
    outs = tuple(jax.ShapeDtypeStruct(shape, dtype) for shape, dtype in outs)
    size = sum(x.size * x.dtype.itemsize for x in list(args) + list(outs))
    return pl.pallas_call(
        kernel,
        out_shape=outs,
        in_specs=specs,
        out_specs=(vmem,) * len(outs),
        scratch_shapes=list(scratch),
        compiler_params=pltpu.CompilerParams(vmem_limit_bytes=limit << 20),
        cost_estimate=pl.CostEstimate(flops=flops, transcendentals=0, bytes_accessed=size),
    )(*args)


def in_hbm(*arrays):
    return [pltpu.with_memory_space_constraint(x, pltpu.HBM) for x in arrays]


def prepare(lens, index, q, do):
    lens, q, do = in_hbm(lens, q, do)
    return call(
        prepare_kernel, (lens, index, q, do),
        ((q.shape, BF16), (do.shape, BF16), ((SPAN, TILE), F32)),
        spaces=[pltpu.HBM, pltpu.SMEM, pltpu.HBM, pltpu.HBM],
        scratch=(
            pltpu.SMEM(lens.shape, jnp.int32),
            pltpu.SemaphoreType.DMA((2, PIECES)),
            pltpu.SemaphoreType.DMA,
        ),
    )


def join_kernel(k_ref, v_ref, out_ref, sems):
    copies = [
        pltpu.make_async_copy(k_ref, out_ref.at[:, KEY], sems.at[0]),
        pltpu.make_async_copy(v_ref, out_ref.at[:, VALUE], sems.at[1]),
    ]
    for copy in copies:
        copy.start()
    for copy in copies:
        copy.wait()


def join(k, v):
    k, v = in_hbm(k, v)
    return call(
        join_kernel, (k, v), (((k.shape[0], 2 * HEAD), BF16),), spaces=[pltpu.HBM] * 2,
        scratch=(pltpu.SemaphoreType.DMA((2,)),),
    )[0]


def score_part(at, qs, dos, kv, bias):
    n = qs.size // HEAD
    return call(
        functools.partial(score_kernel, at), (qs, dos, kv, bias),
        (((CHUNK, n), F32), ((CHUNK, n), F32), ((8, n), F32)), 4 * CHUNK * n * HEAD,
    )


def last_part(at, qs, dos, kv, bias, one, two):
    n = qs.size // HEAD
    return call(
        functools.partial(last_kernel, at), (qs, dos, kv, bias, one, two),
        (((CHUNK, n), F32), ((CHUNK, n), F32), ((8, n), F32)), 4 * CHUNK * n * HEAD,
    )


def grad_part(row, qs, dos, e, dp, stats, dtype):
    n = qs.size // HEAD
    return call(
        functools.partial(grad_kernel, row), (qs, dos, e, dp, stats),
        (((CHUNK, n), BF16), ((CHUNK, n), BF16), ((CHUNK, 2 * HEAD), dtype)),
        4 * CHUNK * n * HEAD,
    )


def query_part(side, scale, kvs, ws, shape):
    n = ws[0].shape[1]
    return call(
        functools.partial(query_kernel, side, scale), (*kvs, *ws), ((shape, BF16),),
        2 * SPAN * n * HEAD, scratch=(pltpu.VMEM((HEAD, SPAN), BF16),),
    )[0]


def per_device(queries, keys, values, output_gradient, doc_lens):
    index = lax.axis_index(SEQ_AXES).astype(jnp.int32).reshape(1)
    own = join(keys, values)
    before = shifted(own, 1)
    qs, dos, bias = prepare(doc_lens, index, queries, output_gradient)
    near = jnp.concatenate([before, own], 0)
    mid = shifted(near, 2)
    far = shifted(near, 4)
    e_near, dp_near, st_near = score_part(2, qs, dos, near, bias)
    e_far, dp_far, st_far = score_part(0, qs, dos, far, bias)
    e_mid, dp_mid, stats = last_part(1, qs, dos, mid, bias, st_near, st_far)
    w_mid, ds_mid, g_mid = grad_part(2, qs, dos, e_mid, dp_mid, stats, BF16)
    from_mid = shifted(g_mid, -2)
    w_far, ds_far, g_far = grad_part(1, qs, dos, e_far, dp_far, stats, BF16)
    from_far = shifted(g_far, -4)
    w_near, ds_near, g_near = grad_part(0, qs, dos, e_near, dp_near, stats, F32)
    kvs = (far, mid, near)
    attended = query_part(VALUE, 1.0, kvs, (w_far, w_mid, w_near), queries.shape)
    attended, from_far, from_mid = lax.optimization_barrier((attended, from_far, from_mid))
    summed = from_far.astype(F32) + from_mid.astype(F32) + g_near
    back = shifted(summed[:TILE].astype(BF16), -1).astype(F32)
    query_grad = query_part(KEY, SCALE, kvs, (ds_far, ds_mid, ds_near), queries.shape)
    total = (summed[TILE:] + back).astype(BF16)
    return attended, query_grad, total[:, :HEAD], total[:, HEAD:]


def solution(mesh):
    rows = P(SEQ_AXES, "tp")
    return jax.shard_map(
        per_device,
        mesh=mesh,
        in_specs=(rows, rows, rows, rows, P()),
        out_specs=(rows, rows, rows, rows),
        check_vma=False,
    )
```

```python
import functools

import jax
import jax.numpy as jnp
from jax import lax
from jax.experimental import pallas as pl
from jax.experimental.pallas import tpu as pltpu
from jax.sharding import PartitionSpec as P

HEAD = 128
TILE = 128
REACH = 5
SPAN = (REACH + 1) * TILE
CHUNK = 2 * TILE
SEQ_AXES = ("dp", "ctx")
SCALE = HEAD ** (-0.5)
LOG2E = 1.4426950408889634
NEG = -1e30
STEP = 2 * TILE
PIECES = 2
KEY, VALUE = pl.ds(0, HEAD), pl.ds(HEAD, HEAD)

NT = (((1,), (1,)), ((), ()))
NN = (((1,), (0,)), ((), ()))
BF16 = jnp.bfloat16
F32 = jnp.float32


def dot(a, b, dims):
    return lax.dot_general(a, b, dims, preferred_element_type=F32)


def shifted(block, distance):
    devices = range(lax.axis_size(SEQ_AXES))
    route = [(i - distance, i) for i in devices if i - distance in devices]
    return lax.ppermute(block, SEQ_AXES, route)


def twice(x):
    return jnp.concatenate([x, x], 1)


def prepare_kernel(
    lens_hbm, index_ref, q_hbm, do_hbm, q_ref, do_ref, bias_ref, lens_ref, sems, lens_sem
):
    lens = pltpu.make_async_copy(lens_hbm, lens_ref, lens_sem)
    lens.start()
    copies = []
    for c in range(PIECES):
        rows = pl.ds(c * (TILE // PIECES), TILE // PIECES)
        for x, (src, dst) in enumerate(((q_hbm, q_ref), (do_hbm, do_ref))):
            copies.append(
                pltpu.make_async_copy(src.at[rows, :], dst.at[rows, :], sems.at[x, c])
            )
            copies[-1].start()
    lens.wait()
    base = (index_ref[0] - REACH) * TILE
    q_pos = base + REACH * TILE + lax.broadcasted_iota(jnp.int32, (8, TILE), 1)
    doc_start = jnp.zeros((8, TILE), jnp.int32)
    end = jnp.int32(0)
    for i in range(lens_ref.shape[0]):
        end = end + lens_ref[i]
        doc_start = jnp.where(q_pos >= end, jnp.maximum(doc_start, end), doc_start)
    q_pos, doc_start = q_pos[:1], doc_start[:1]
    for t in range(REACH + 1):
        k_pos = base + t * TILE + lax.broadcasted_iota(jnp.int32, (TILE, TILE), 0)
        seen = (k_pos >= doc_start) & (k_pos <= q_pos)
        bias_ref[pl.ds(t * TILE, TILE), :] = jnp.where(seen, 0.0, NEG)
    for copy in copies:
        copy.wait()


def stacked(ref, heads):
    return jnp.concatenate([ref[:, pl.ds(h * HEAD, HEAD)] for h in heads], 0)


def scores(qs_ref, dos_ref, kv_ref, bias_ref, at, part):
    heads = (part.start // HEAD, part.start // HEAD + 1)
    dp = dot(kv_ref[:, HEAD:], stacked(dos_ref, heads), NT)
    s = dot(kv_ref[:, :HEAD], stacked(qs_ref, heads), NT) * (SCALE * LOG2E)
    s = s + twice(bias_ref[pl.ds(at * CHUNK, CHUNK), :])
    m = jnp.max(s, axis=0, keepdims=True)
    e = jnp.exp2(s - m)
    total = jnp.sum(e, axis=0, keepdims=True)
    return e, dp, m, total, jnp.sum(e * dp, axis=0, keepdims=True)


def parts_of(qs_ref):
    return [pl.ds(j * STEP, STEP) for j in range(qs_ref.shape[1] // STEP)]


def score_kernel(at, qs_ref, dos_ref, kv_ref, bias_ref, e_ref, dp_ref, stats_ref):
    for part in parts_of(qs_ref):
        e, dp, m, total, delta = scores(qs_ref, dos_ref, kv_ref, bias_ref, at, part)
        e_ref[:, part] = e
        dp_ref[:, part] = dp
        stats_ref[0:1, part] = m
        stats_ref[1:2, part] = total
        stats_ref[2:3, part] = delta


def grads(qs_ref, dos_ref, w_ref, ds_ref, out_ref):
    heads = range(qs_ref.shape[1] // HEAD)
    out_ref[:, :HEAD] = (dot(ds_ref[...], stacked(qs_ref, heads), NN) * SCALE).astype(out_ref.dtype)
    out_ref[:, HEAD:] = dot(w_ref[...], stacked(dos_ref, heads), NN).astype(out_ref.dtype)


def last_kernel(
    at, qs_ref, dos_ref, kv_ref, bias_ref, one_ref, two_ref, e_ref, dp_ref, stats_ref
):
    for part in parts_of(qs_ref):
        e, dp, m, total, delta = scores(qs_ref, dos_ref, kv_ref, bias_ref, at, part)
        e_ref[:, part] = e
        dp_ref[:, part] = dp
        m_one, m_two = one_ref[0:1, part], two_ref[0:1, part]
        top = jnp.maximum(m, jnp.maximum(m_one, m_two))
        a, a_one, a_two = (jnp.exp2(x - top) for x in (m, m_one, m_two))
        total = a * total + a_one * one_ref[1:2, part] + a_two * two_ref[1:2, part]
        delta = a * delta + a_one * one_ref[2:3, part] + a_two * two_ref[2:3, part]
        r = 1.0 / total
        stats_ref[0:1, part] = a_one * r
        stats_ref[1:2, part] = a_two * r
        stats_ref[2:3, part] = a * r
        stats_ref[3:4, part] = delta * r


def grad_kernel(row, qs_ref, dos_ref, e_ref, dp_ref, stats_ref, w_ref, ds_ref, out_ref):
    for part in parts_of(qs_ref):
        p = e_ref[:, part] * stats_ref[row : row + 1, part]
        w_ref[:, part] = p.astype(BF16)
        ds_ref[:, part] = (p * (dp_ref[:, part] - stats_ref[3:4, part])).astype(BF16)
    grads(qs_ref, dos_ref, w_ref, ds_ref, out_ref)


def query_kernel(far_ref, mid_ref, near_ref, *refs):
    ws, dss, (o_ref, dq_ref, t_ref) = refs[:3], refs[3:6], refs[6:]
    for t, ref in enumerate((far_ref, mid_ref, near_ref)):
        t_ref[:, pl.ds(t * CHUNK, CHUNK)] = ref[...].T
    for j, part in enumerate(pl.ds(j * STEP, STEP) for j in range(ws[0].shape[1] // STEP)):
        w = jnp.concatenate([ref[:, part] for ref in ws], 0)
        ds = jnp.concatenate([ref[:, part] for ref in dss], 0)
        o = dot(t_ref[HEAD:, :], w, NN).astype(BF16)
        dq = (dot(t_ref[:HEAD, :], ds, NN) * SCALE).astype(BF16)
        for x, ref in ((o, o_ref), (dq, dq_ref)):
            ref[:, pl.ds(j * STEP, HEAD)] = x[:, :TILE].T
            ref[:, pl.ds(j * STEP + HEAD, HEAD)] = x[:, TILE:].T


def call(kernel, args, outs, flops=0, scratch=(), spaces=None, limit=16):
    vmem = pl.BlockSpec(memory_space=pltpu.VMEM)
    specs = [pl.BlockSpec(memory_space=s) for s in spaces or [pltpu.VMEM] * len(args)]
    outs = tuple(jax.ShapeDtypeStruct(shape, dtype) for shape, dtype in outs)
    size = sum(x.size * x.dtype.itemsize for x in list(args) + list(outs))
    return pl.pallas_call(
        kernel,
        out_shape=outs,
        in_specs=specs,
        out_specs=(vmem,) * len(outs),
        scratch_shapes=list(scratch),
        compiler_params=pltpu.CompilerParams(vmem_limit_bytes=limit << 20),
        cost_estimate=pl.CostEstimate(flops=flops, transcendentals=0, bytes_accessed=size),
    )(*args)


def in_hbm(*arrays):
    return [pltpu.with_memory_space_constraint(x, pltpu.HBM) for x in arrays]


def prepare(lens, index, q, do):
    lens, q, do = in_hbm(lens, q, do)
    return call(
        prepare_kernel, (lens, index, q, do),
        ((q.shape, BF16), (do.shape, BF16), ((SPAN, TILE), F32)),
        spaces=[pltpu.HBM, pltpu.SMEM, pltpu.HBM, pltpu.HBM],
        scratch=(
            pltpu.SMEM(lens.shape, jnp.int32),
            pltpu.SemaphoreType.DMA((2, PIECES)),
            pltpu.SemaphoreType.DMA,
        ),
    )


def join_kernel(k_ref, v_ref, out_ref, sems):
    copies = [
        pltpu.make_async_copy(k_ref, out_ref.at[:, KEY], sems.at[0]),
        pltpu.make_async_copy(v_ref, out_ref.at[:, VALUE], sems.at[1]),
    ]
    for copy in copies:
        copy.start()
    for copy in copies:
        copy.wait()


def join(k, v):
    k, v = in_hbm(k, v)
    return call(
        join_kernel, (k, v), (((k.shape[0], 2 * HEAD), BF16),), spaces=[pltpu.HBM] * 2,
        scratch=(pltpu.SemaphoreType.DMA((2,)),),
    )[0]


def score_part(at, qs, dos, kv, bias):
    n = qs.size // HEAD
    return call(
        functools.partial(score_kernel, at), (qs, dos, kv, bias),
        (((CHUNK, n), F32), ((CHUNK, n), F32), ((8, n), F32)), 4 * CHUNK * n * HEAD,
    )


def last_part(at, qs, dos, kv, bias, one, two):
    n = qs.size // HEAD
    return call(
        functools.partial(last_kernel, at), (qs, dos, kv, bias, one, two),
        (((CHUNK, n), F32), ((CHUNK, n), F32), ((8, n), F32)), 4 * CHUNK * n * HEAD,
    )


def grad_part(row, qs, dos, e, dp, stats, dtype):
    n = qs.size // HEAD
    return call(
        functools.partial(grad_kernel, row), (qs, dos, e, dp, stats),
        (((CHUNK, n), BF16), ((CHUNK, n), BF16), ((CHUNK, 2 * HEAD), dtype)),
        4 * CHUNK * n * HEAD,
    )


def query_part(kvs, ws, dss, shape):
    n = ws[0].shape[1]
    return call(
        query_kernel, (*kvs, *ws, *dss), ((shape, BF16), (shape, BF16)),
        4 * SPAN * n * HEAD, scratch=(pltpu.VMEM((2 * HEAD, SPAN), BF16),),
    )


def per_device(queries, keys, values, output_gradient, doc_lens):
    index = lax.axis_index(SEQ_AXES).astype(jnp.int32).reshape(1)
    own = join(keys, values)
    before = shifted(own, 1)
    qs, dos, bias = prepare(doc_lens, index, queries, output_gradient)
    near = jnp.concatenate([before, own], 0)
    mid = shifted(near, 2)
    far = shifted(near, 4)
    e_near, dp_near, st_near = score_part(2, qs, dos, near, bias)
    e_far, dp_far, st_far = score_part(0, qs, dos, far, bias)
    e_mid, dp_mid, stats = last_part(1, qs, dos, mid, bias, st_near, st_far)
    w_mid, ds_mid, g_mid = grad_part(2, qs, dos, e_mid, dp_mid, stats, BF16)
    from_mid = shifted(g_mid, -2)
    w_far, ds_far, g_far = grad_part(1, qs, dos, e_far, dp_far, stats, BF16)
    from_far = shifted(g_far, -4)
    w_near, ds_near, g_near = grad_part(0, qs, dos, e_near, dp_near, stats, F32)
    attended, query_grad = query_part(
        (far, mid, near), (w_far, w_mid, w_near), (ds_far, ds_mid, ds_near), queries.shape
    )
    attended, query_grad, from_far, from_mid = lax.optimization_barrier(
        (attended, query_grad, from_far, from_mid)
    )
    summed = from_far.astype(F32) + from_mid.astype(F32) + g_near
    back = shifted(summed[:TILE].astype(BF16), -1).astype(F32)
    total = (summed[TILE:] + back).astype(BF16)
    return attended, query_grad, total[:, :HEAD], total[:, HEAD:]


def solution(mesh):
    rows = P(SEQ_AXES, "tp")
    return jax.shard_map(
        per_device,
        mesh=mesh,
        in_specs=(rows, rows, rows, rows, P()),
        out_specs=(rows, rows, rows, rows),
        check_vma=False,
    )
```
